512 devices in a mesh: gx: 16 (over z), gy: 32 (over x, y, core).
Axes of the slice: x: 4, y: 4, z: 16, core: 2. Of those that a mesh axis runs over, the one named last changes fastest.
Arguments:
- tokens: bfloat16 [768, 16384], P('gy', 'gx'), may hold values from -6 to 6
- gate_weight: bfloat16 [16384, 26624], P('gx', 'gy'), may hold values from -0.046875 to 0.046875
- up_weight: bfloat16 [16384, 26624], P('gx', 'gy'), may hold values from -0.046875 to 0.046875
- down_weight: bfloat16 [26624, 16384], P('gy', 'gx'), may hold values from -0.0390625 to 0.0390625
Outputs:
- mixed: bfloat16 [768, 16384], P('gy', 'gx')
The draws below stay inside these ranges and needn't reach their ends.
All inputs are finite; a program needn't handle non-finite values.
Results may differ from the reference program's by a relative error of at most 0.005.
Values may be sent and summed in bfloat16 or wider, within the bound.
No kernel may reach another device: no remote copies, remote signals or barrier semaphores. Data moves between devices by JAX's collectives and lax.ppermute only.
A program may use at most 64 MiB of HBM per device.

```python
import jax
import jax.numpy as jnp

D = 16384
FF = 26624
TOKENS = 768


def steps_of(own_key, shape, split, low, high):
    gain, own = 1.0, jax.random.fold_in(own_key, 6)
    for position, parts in split:
        steps = jnp.exp(jax.random.uniform(jax.random.fold_in(own, position), (parts,), jnp.float32, low / len(split), high / len(split)))
        gain = gain * jnp.repeat(steps, shape[position] // parts).reshape([-1 if axis == position else 1 for axis in range(len(shape))])
    return gain


def noise(rng, shape, width, limit, split=(), held_as=jnp.bfloat16):
    loudness = steps_of(rng, shape, split, -0.22, 0.18) if split else 1.0
    drawn = jax.random.normal(rng, shape, jnp.float32) * width * loudness
    return jnp.minimum(jnp.maximum(drawn, -limit), limit).astype(held_as)


def setup_inputs(seed: int = 0) -> dict:
    arg_keys = jax.random.split(jax.random.key(seed), 5)
    tokens = noise(arg_keys[0], (TOKENS, D), 1.0, 6.0, ((0, 32), (1, 16)))
    gate_weight = noise(arg_keys[1], (D, FF), D ** -0.5, 0.046875, ((0, 16), (1, 32)))
    up_weight = noise(arg_keys[2], (D, FF), D ** -0.5, 0.046875, ((0, 16), (1, 32)))
    down_weight = noise(arg_keys[3], (FF, D), FF ** -0.5, 0.0390625, ((0, 32), (1, 16)))
    return dict(tokens=tokens, gate_weight=gate_weight, up_weight=up_weight, down_weight=down_weight)


def reference(tokens, gate_weight, up_weight, down_weight):
    gate = jnp.dot(tokens, gate_weight, preferred_element_type=jnp.float32)
    up = jnp.dot(tokens, up_weight, preferred_element_type=jnp.float32)
    hidden = (jax.nn.silu(gate) * up).astype(jnp.bfloat16)
    total = jnp.dot(hidden, down_weight, preferred_element_type=jnp.float32)
    return total.astype(jnp.bfloat16)
```

```python
import jax
import jax.numpy as jnp
from jax import lax
from jax.sharding import PartitionSpec as P

F32, F16, BF16 = jnp.float32, jnp.float16, jnp.bfloat16
LOW = 2.0**-100


def dot(a, b, dims):
    return lax.dot_general(a, b, (dims, ((), ())), preferred_element_type=F32)


def gather_hidden(hidden):
    rows, columns = hidden.shape
    wide = hidden.astype(F32)
    power = jnp.ceil(jnp.log2(jnp.maximum(jnp.max(jnp.abs(wide), axis=0, keepdims=True), LOW)))
    scaled = jnp.concatenate([wide * jnp.exp2(14.0 - power), power], axis=0).astype(F16)
    parts = lax.all_gather(scaled, "gx", axis=0).astype(F32)
    whole = parts[:, :rows] * jnp.exp2(parts[:, rows:] - 14.0)
    return whole.astype(BF16).reshape(-1, columns)


def local(tokens, gate_weight, up_weight, down_weight):
    peers = lax.axis_size("gy")
    count = tokens.shape[0]
    total = peers * count
    copies = jnp.broadcast_to(tokens[None], (peers,) + tokens.shape)
    piece = lax.all_to_all(copies, "gy", 0, 0, tiled=True).reshape(total, -1)
    gate_term = dot(gate_weight, piece, ((0,), (1,)))
    up_term = dot(up_weight, piece, ((0,), (1,)))
    summed = lax.psum_scatter(
        jnp.concatenate([gate_term, up_term], axis=1), "gx", scatter_dimension=0, tiled=True
    )
    summed = lax.optimization_barrier(summed)
    hidden = (jax.nn.silu(summed[:, :total]) * summed[:, total:]).astype(BF16)
    whole = gather_hidden(hidden)
    terms = dot(whole, down_weight, ((0,), (0,))).astype(BF16).reshape(peers, count, -1)
    received = lax.all_to_all(terms, "gy", 0, 0, tiled=True)
    return jnp.sum(received.astype(F32), axis=0).astype(BF16)


def solution(mesh):
    in_specs = (P("gy", "gx"), P("gx", "gy"), P("gx", "gy"), P("gy", "gx"))
    return jax.shard_map(local, mesh=mesh, in_specs=in_specs, out_specs=P("gy", "gx"), check_vma=False)
```

```python
import jax
import jax.numpy as jnp
from jax import lax
from jax.sharding import PartitionSpec as P

F32, F16, BF16 = jnp.float32, jnp.float16, jnp.bfloat16
LOW = 2.0**-100


def dot(a, b, dims):
    return lax.dot_general(a, b, (dims, ((), ())), preferred_element_type=F32)


def gather_hidden(hidden):
    rows, columns = hidden.shape
    wide = hidden.astype(F32)
    power = jnp.ceil(jnp.log2(jnp.maximum(jnp.max(jnp.abs(wide), axis=0, keepdims=True), LOW)))
    scaled = jnp.concatenate([wide * jnp.exp2(14.0 - power), power], axis=0).astype(F16)
    parts = lax.all_gather(scaled, "gx", axis=0).astype(F32)
    whole = parts[:, :rows] * jnp.exp2(parts[:, rows:] - 14.0)
    return whole.astype(BF16).reshape(-1, columns)


def local(tokens, gate_weight, up_weight, down_weight):
    peers = lax.axis_size("gy")
    count = tokens.shape[0]
    half = peers // 2 * count
    same = [[2 * i + core for i in range(peers // 2)] for core in range(2)]
    swap = [(i, i ^ 1) for i in range(peers)]
    copies = jnp.broadcast_to(tokens[None], (peers // 2,) + tokens.shape)
    own = lax.all_to_all(copies, "gy", 0, 0, axis_index_groups=same, tiled=True).reshape(half, -1)
    other = lax.ppermute(own, "gy", swap)
    terms = [dot(w, t, ((0,), (1,))) for w in (gate_weight, up_weight) for t in (own, other)]
    summed = lax.psum_scatter(jnp.concatenate(terms, axis=1), "gx", scatter_dimension=0, tiled=True)
    summed = lax.optimization_barrier(summed)
    hidden = (jax.nn.silu(summed[:, : 2 * half]) * summed[:, 2 * half :]).astype(BF16)
    whole = gather_hidden(hidden)
    away = dot(whole[:, half:], down_weight, ((0,), (0,))).astype(BF16)
    away = lax.ppermute(away, "gy", swap)
    kept = dot(whole[:, :half], down_weight, ((0,), (0,)))
    mine = (kept + away.astype(F32)).astype(BF16).reshape(peers // 2, count, -1)
    received = lax.all_to_all(mine, "gy", 0, 0, axis_index_groups=same, tiled=True)
    return jnp.sum(received.astype(F32), axis=0).astype(BF16)


def solution(mesh):
    in_specs = (P("gy", "gx"), P("gx", "gy"), P("gx", "gy"), P("gy", "gx"))
    return jax.shard_map(local, mesh=mesh, in_specs=in_specs, out_specs=P("gy", "gx"), check_vma=False)
```

```python
import jax
import jax.numpy as jnp
from jax import lax
from jax.sharding import PartitionSpec as P

F32, F16, BF16 = jnp.float32, jnp.float16, jnp.bfloat16
LOW = 2.0**-100
TILE = 8


def dot(a, b, dims):
    return lax.dot_general(a, b, (dims, ((), ())), preferred_element_type=F32)


def gather_hidden(hidden):
    rows, columns = hidden.shape
    wide = hidden.astype(F32)
    power = jnp.ceil(jnp.log2(jnp.maximum(jnp.max(jnp.abs(wide), axis=0, keepdims=True), LOW)))
    scaled = jnp.concatenate([wide * jnp.exp2(14.0 - power), power], axis=0).astype(F16)
    parts = lax.all_gather(scaled, "gx", axis=0).astype(F32)
    whole = parts[:, :rows] * jnp.exp2(parts[:, rows:] - 14.0)
    return whole.astype(BF16).reshape(-1, columns)


def local(tokens, gate_weight, up_weight, down_weight):
    parts, peers = lax.axis_size("gx"), lax.axis_size("gy")
    units = gate_weight.shape[1]
    count = tokens.shape[0]
    half = peers // 2 * count
    same = [[2 * i + core for i in range(peers // 2)] for core in range(2)]
    swap = [(i, i ^ 1) for i in range(peers)]
    copies = jnp.broadcast_to(tokens[None], (peers // 2,) + tokens.shape)
    own = lax.all_to_all(copies, "gy", 0, 0, axis_index_groups=same, tiled=True).reshape(half, -1)
    other = lax.ppermute(own, "gy", swap)
    terms = [dot(w, t, ((0,), (1,))) for w in (gate_weight, up_weight) for t in (own, other)]
    share = -(-units // parts // TILE) * TILE - 1
    joined = jnp.pad(jnp.concatenate(terms, axis=1), ((0, parts * share - units), (0, 0)))
    summed = lax.psum_scatter(joined, "gx", scatter_dimension=0, tiled=True)
    summed = lax.optimization_barrier(summed)
    hidden = (jax.nn.silu(summed[:, : 2 * half]) * summed[:, 2 * half :]).astype(BF16)
    whole = gather_hidden(hidden)[:units]
    away = dot(whole[:, half:], down_weight, ((0,), (0,))).astype(BF16)
    away = lax.ppermute(away, "gy", swap)
    kept = dot(whole[:, :half], down_weight, ((0,), (0,)))
    mine = (kept + away.astype(F32)).astype(BF16).reshape(peers // 2, count, -1)
    received = lax.all_to_all(mine, "gy", 0, 0, axis_index_groups=same, tiled=True)
    return jnp.sum(received.astype(F32), axis=0).astype(BF16)


def solution(mesh):
    in_specs = (P("gy", "gx"), P("gx", "gy"), P("gx", "gy"), P("gy", "gx"))
    return jax.shard_map(local, mesh=mesh, in_specs=in_specs, out_specs=P("gy", "gx"), check_vma=False)
```

```python
import jax
import jax.numpy as jnp
from jax import lax
from jax.sharding import PartitionSpec as P

F32, F16, BF16 = jnp.float32, jnp.float16, jnp.bfloat16
LOW = 2.0**-100
TILE = 8
LANES = 128


def dot(a, b, dims):
    return lax.dot_general(a, b, (dims, ((), ())), preferred_element_type=F32)


def gather_hidden(hidden):
    rows, columns = hidden.shape
    wide = hidden.astype(F32)
    power = jnp.ceil(jnp.log2(jnp.maximum(jnp.max(jnp.abs(wide), axis=0, keepdims=True), LOW)))
    scaled = jnp.concatenate([wide * jnp.exp2(14.0 - power), power], axis=0).astype(F16)
    parts = lax.all_gather(scaled, "gx", axis=0).astype(F32)
    whole = parts[:, :rows] * jnp.exp2(parts[:, rows:] - 14.0)
    return whole.astype(BF16).reshape(-1, columns)


def local(tokens, gate_weight, up_weight, down_weight):
    parts, peers = lax.axis_size("gx"), lax.axis_size("gy")
    units = gate_weight.shape[1]
    count = tokens.shape[0]
    half = peers // 2 * count
    blocks = half // LANES
    same = [[2 * i + core for i in range(peers // 2)] for core in range(2)]
    swap = [(i, i ^ 1) for i in range(peers)]
    copies = jnp.broadcast_to(tokens[None], (peers // 2,) + tokens.shape)
    own = lax.all_to_all(copies, "gy", 0, 0, axis_index_groups=same, tiled=True).reshape(half, -1)
    other = lax.ppermute(own, "gy", swap)
    rows = []
    for part in (own, other):
        gate, up = (dot(w, part, ((0,), (1,))) for w in (gate_weight, up_weight))
        for block in range(blocks):
            columns = slice(block * LANES, (block + 1) * LANES)
            rows.append(jnp.concatenate([gate[:, columns], up[:, columns]], axis=1))
    total = 2 * blocks * units
    share = -(-total // parts // TILE) * TILE
    share = share - 1 if parts * (share - 1) >= total else share + TILE - 1
    joined = jnp.pad(jnp.concatenate(rows, axis=0), ((0, parts * share - total), (0, 0)))
    summed = lax.psum_scatter(joined, "gx", scatter_dimension=0, tiled=True)
    summed = lax.optimization_barrier(summed)
    hidden = (jax.nn.silu(summed[:, :LANES]) * summed[:, LANES:]).astype(BF16)
    whole = gather_hidden(hidden)
    whole = jnp.concatenate([whole[i * units : (i + 1) * units] for i in range(2 * blocks)], axis=1)
    away, kept = (dot(t, down_weight, ((0,), (0,))) for t in (whole[:, half:], whole[:, :half]))
    away = lax.ppermute(away.astype(BF16), "gy", swap)
    mine = (kept + away.astype(F32)).astype(BF16).reshape(peers // 2, count, -1)
    received = lax.all_to_all(mine, "gy", 0, 0, axis_index_groups=same, tiled=True)
    return jnp.sum(received.astype(F32), axis=0).astype(BF16)


def solution(mesh):
    in_specs = (P("gy", "gx"), P("gx", "gy"), P("gx", "gy"), P("gy", "gx"))
    return jax.shard_map(local, mesh=mesh, in_specs=in_specs, out_specs=P("gy", "gx"), check_vma=False)
```

```python
import jax
import jax.numpy as jnp
from jax import lax
from jax.sharding import PartitionSpec as P

F32, F16, BF16 = jnp.float32, jnp.float16, jnp.bfloat16
LOW = 2.0**-100
TILE = 8
LANES = 128


def dot(a, b, dims):
    return lax.dot_general(a, b, (dims, ((), ())), preferred_element_type=F32)


def gather_hidden(hidden):
    rows = hidden.shape[0]
    wide = hidden.astype(F32)
    power = jnp.ceil(jnp.log2(jnp.maximum(jnp.max(jnp.abs(wide), axis=0, keepdims=True), LOW)))
    scaled = jnp.concatenate([wide * jnp.exp2(14.0 - power), power], axis=0).astype(F16)
    parts = lax.all_gather(scaled, "gx", axis=0).astype(F32)
    return (parts * jnp.exp2(parts[:, rows:] - 14.0)).astype(BF16)


def local(tokens, gate_weight, up_weight, down_weight):
    parts, peers = lax.axis_size("gx"), lax.axis_size("gy")
    units = gate_weight.shape[1]
    count = tokens.shape[0]
    half = peers // 2 * count
    blocks = half // LANES
    same = [[2 * i + core for i in range(peers // 2)] for core in range(2)]
    swap = [(i, i ^ 1) for i in range(peers)]
    copies = jnp.broadcast_to(tokens[None], (peers // 2,) + tokens.shape)
    own = lax.all_to_all(copies, "gy", 0, 0, axis_index_groups=same, tiled=True).reshape(half, -1)
    other = lax.ppermute(own, "gy", swap)
    rows = []
    for part in (own, other):
        gate, up = (dot(w, part, ((0,), (1,))) for w in (gate_weight, up_weight))
        for block in range(blocks):
            columns = slice(block * LANES, (block + 1) * LANES)
            rows.append(jnp.concatenate([gate[:, columns], up[:, columns]], axis=1))
    total = 2 * blocks * units
    share = -(-total // parts // TILE) * TILE
    share = share - 1 if parts * (share - 1) >= total else share + TILE - 1
    joined = jnp.pad(jnp.concatenate(rows, axis=0), ((0, parts * share - total), (0, 0)))
    summed = lax.psum_scatter(joined, "gx", scatter_dimension=0, tiled=True)
    summed = lax.optimization_barrier(summed)
    hidden = (jax.nn.silu(summed[:, :LANES]) * summed[:, LANES:]).astype(BF16)
    whole = gather_hidden(hidden)

    def block(i):
        spans = []
        for z in range(parts):
            first, end = max(i * units, z * share), min((i + 1) * units, (z + 1) * share)
            if first < end:
                spans.append(whole[z, first - z * share : end - z * share])
        return jnp.concatenate(spans, axis=0)

    def down(first):
        return dot(jnp.concatenate([block(first + i) for i in range(blocks)], axis=1), down_weight, ((0,), (0,)))

    away, kept = down(blocks), down(0)
    away = lax.ppermute(away.astype(BF16), "gy", swap)
    mine = (kept + away.astype(F32)).astype(BF16).reshape(peers // 2, count, -1)
    received = lax.all_to_all(mine, "gy", 0, 0, axis_index_groups=same, tiled=True)
    return jnp.sum(received.astype(F32), axis=0).astype(BF16)


def solution(mesh):
    in_specs = (P("gy", "gx"), P("gx", "gy"), P("gx", "gy"), P("gy", "gx"))
    return jax.shard_map(local, mesh=mesh, in_specs=in_specs, out_specs=P("gy", "gx"), check_vma=False)
```

```python
import jax
import jax.numpy as jnp
from jax import lax
from jax.sharding import PartitionSpec as P

F32, F16, BF16 = jnp.float32, jnp.float16, jnp.bfloat16
LOW = 2.0**-100
TILE = 8
LANES = 128


def dot(a, b, dims):
    return lax.dot_general(a, b, (dims, ((), ())), preferred_element_type=F32)


def gather_hidden(hidden):
    rows = hidden.shape[0]
    wide = hidden.astype(F32)
    power = jnp.ceil(jnp.log2(jnp.maximum(jnp.max(jnp.abs(wide), axis=0, keepdims=True), LOW)))
    scaled = jnp.concatenate([wide * jnp.exp2(14.0 - power), power], axis=0).astype(F16)
    parts = lax.all_gather(scaled, "gx", axis=0).astype(F32)
    return (parts * jnp.exp2(parts[:, rows:] - 14.0)).astype(BF16)


def local(tokens, gate_weight, up_weight, down_weight):
    parts, peers = lax.axis_size("gx"), lax.axis_size("gy")
    units = gate_weight.shape[1]
    count = tokens.shape[0]
    half = peers // 2 * count
    blocks = half // LANES
    same = [[2 * i + core for i in range(peers // 2)] for core in range(2)]
    swap = [(i, i ^ 1) for i in range(peers)]
    copies = jnp.broadcast_to(tokens[None], (peers // 2,) + tokens.shape)
    own = lax.all_to_all(copies, "gy", 0, 0, axis_index_groups=same, tiled=True).reshape(half, -1)
    other = lax.ppermute(own, "gy", swap)
    rows = []
    for part in (own, other):
        gate, up = (dot(w, part, ((0,), (1,))) for w in (gate_weight, up_weight))
        for block in range(blocks):
            columns = slice(block * LANES, (block + 1) * LANES)
            rows.append(jnp.concatenate([gate[:, columns], up[:, columns]], axis=1))
    total = 2 * blocks * units
    share = -(-total // parts // TILE) * TILE
    share = share - 1 if parts * (share - 1) >= total else share + TILE - 1
    joined = jnp.pad(jnp.concatenate(rows, axis=0), ((0, parts * share - total), (0, 0)))
    summed = lax.psum_scatter(joined, "gx", scatter_dimension=0, tiled=True)
    summed = lax.optimization_barrier(summed)
    hidden = (jax.nn.silu(summed[:, :LANES]) * summed[:, LANES:]).astype(BF16)
    whole = gather_hidden(hidden)

    def block(i):
        spans = []
        for z in range(parts):
            first, end = max(i * units, z * share), min((i + 1) * units, (z + 1) * share)
            if first < end:
                spans.append(whole[z, first - z * share : end - z * share])
        return jnp.concatenate(spans, axis=0)

    def down(first):
        return dot(jnp.concatenate([block(first + i) for i in range(blocks)], axis=1), down_weight, ((0,), (0,)))

    away = lax.ppermute(down(blocks).astype(BF16), "gy", swap)
    kept = lax.optimization_barrier(down(0))
    mine = (kept + away.astype(F32)).astype(BF16).reshape(peers // 2, count, -1)
    received = lax.all_to_all(mine, "gy", 0, 0, axis_index_groups=same, tiled=True)
    return jnp.sum(received.astype(F32), axis=0).astype(BF16)


def solution(mesh):
    in_specs = (P("gy", "gx"), P("gx", "gy"), P("gx", "gy"), P("gy", "gx"))
    return jax.shard_map(local, mesh=mesh, in_specs=in_specs, out_specs=P("gy", "gx"), check_vma=False)
```
